32 devices in a mesh: dp: 8 (over y, x, core), mp: 4 (over z).
Axes of the slice: x: 2, y: 2, z: 4, core: 2. Of those that a mesh axis runs over, the one named last changes fastest.
Arguments:
- reservoir: bfloat16 [32768, 1024], P('dp'), may hold values from -6 to 6
- pull_list: int32 [8, 8, 1], P(None, 'dp'), may hold values from 0 to 31
- pull_counts: int32 [8, 8], P('dp'), may hold values from 0 to 1, as said below
- first_pattern: int32 [64, 2], P('mp'), may hold values from 0 to 7, all different within a row
- first_weight: bfloat16 [64, 2, 128, 128], P('mp'), may hold values from -0.375 to 0.375
- first_bias: float32 [8192], P('mp'), may hold values from -3 to 3
- second_pattern: int32 [64, 16], P('mp'), may hold values from 0 to 63, all different within a row
- second_weight: bfloat16 [64, 16, 128, 128], P('mp'), may hold values from -0.125 to 0.125
- cotangent: bfloat16 [4096, 8192], P('dp', 'mp'), may hold values from -0.09375 to 0.09375
Outputs:
- second_out: bfloat16 [4096, 8192], P('dp', 'mp')
- first_grad: float32 [64, 32768], P('mp', 'dp')
- second_grad: float32 [64, 262144], P('mp', 'dp')
- bias_grad: float32 [8192], P('mp')
The draws below stay inside these ranges and needn't reach their ends.
Inputs may be any that keep to these rules, and one draw needn't show every extreme that they name: `pull_list`: only slots s below pull_counts[r, o] are used; others hold valid block numbers that are ignored. `pull_counts`: every row sums to 4; one owner gives 1 block to every requester.
All inputs are finite; a program needn't handle non-finite values.
Results may differ from the reference program's by a relative error of at most 0.019.
Values may be sent and summed in bfloat16 or wider, within the bound.
A program may use at most 128 MiB of HBM per device.

```python
import jax
import jax.numpy as jnp
from jax import lax

BLOCK = 128
DIN = 1024
H = 8192
CAP = 1
BLK_DEV = 4
OWN = 32
ROWS = 512
BATCH = 4096
RES_ROWS = 32768
CB = 64
IB1 = 8
KEEP1 = 2
KEEP2 = 16
N_DP = 8
N_MP = 4


def draw_pull_counts(key, part):
    slots = N_DP * CAP
    hot = jax.random.randint(jax.random.fold_in(key, 11), (), 0, N_DP)
    favour = jax.random.randint(jax.random.fold_in(key, 12), (N_DP,), 0, 4)
    noise = jax.random.randint(jax.random.fold_in(key, 13), (N_DP, slots), 0, 65536)
    position = jnp.arange(slots, dtype=jnp.int32)
    owner = position // CAP
    level = jnp.where(owner == hot, 4, favour[owner])
    score = (level[None, :] * 65536 + noise) * slots + position[None, :]
    top_vals, chosen = lax.top_k(score, BLK_DEV)
    taken = jnp.sum((chosen[:, :, None] == position[None, None, :]).astype(jnp.int32), axis=1)
    return jnp.sum(taken.reshape(N_DP, N_DP, CAP), axis=2).astype(jnp.int32)


def set_ends(array, rng, smallest, top_value):
    spot = [jax.random.randint(jax.random.fold_in(rng, axis), (), 0, length) for axis, length in enumerate(array.shape)]
    longest = array.shape.index(max(array.shape))
    neighbour = spot[:longest] + [(spot[longest] + 1) % array.shape[longest]] + spot[longest + 1:]
    return array.at[tuple(spot)].set(smallest).at[tuple(neighbour)].set(top_value)


def shard_levels(rng, extent, pieces, smallest, top_value):
    def one(axis_at, shards_of):
        steps = jax.random.uniform(jax.random.fold_in(jax.random.fold_in(rng, 6), axis_at), (shards_of,), jnp.float32, smallest / len(pieces), top_value / len(pieces))
        return jnp.repeat(jnp.exp(steps), extent[axis_at] // shards_of).reshape((-1,) + (1,) * (len(extent) - axis_at - 1))

    gain = one(*pieces[0])
    for cut in pieces[1:]:
        gain = gain * one(*cut)
    return gain


def picks_of(own_key, rows, count, top, lift):
    order = jax.random.permutation(jax.random.fold_in(own_key, 1), count)
    boost = order
    for power in range(3):
        boost = boost * boost // count
    boost = boost * lift // count
    lots = jax.random.randint(jax.random.fold_in(own_key, 2), (rows, count), 0, 4096) + boost
    fixed_rows = jax.random.permutation(jax.random.fold_in(own_key, 3), rows)[jnp.arange(count) % rows]
    lots = jnp.where(jnp.arange(rows)[:, None] == fixed_rows[None, :], 1 << 14, lots)
    merit = lots * count + jnp.arange(count)
    return lax.top_k(merit.astype(jnp.int32), top)[1].astype(jnp.int32)


def centred(key, dims, deviation, limit, shards=(), kind=jnp.bfloat16):
    values = jax.random.normal(key, dims, jnp.float32) * deviation
    if len(shards) > 0:
        values = shard_levels(key, dims, shards, -0.22, 0.18) * values
    return jnp.clip(values, min=-limit, max=limit).astype(kind)


def setup_inputs(seed: int = 0) -> dict:
    arg_keys = jax.random.split(jax.random.key(seed), 10)
    return {
        "reservoir": centred(arg_keys[0], (RES_ROWS, DIN), 1.0, 6.0, ((0, 8),)),
        "pull_list": set_ends(jax.random.randint(arg_keys[1], (N_DP, N_DP, CAP), 0, OWN), jax.random.fold_in(arg_keys[1], 1), 0, OWN - 1).astype(jnp.int32),
        "pull_counts": draw_pull_counts(jax.random.fold_in(arg_keys[9], 71), 0),
        "first_pattern": picks_of(arg_keys[3], CB, IB1, KEEP1, 0),
        "first_weight": centred(arg_keys[4], (CB, KEEP1, BLOCK, BLOCK), (KEEP1 * BLOCK) ** -0.5, 0.375, ((0, 4),)),
        "first_bias": centred(arg_keys[5], (H,), 0.5, 3.0, ((0, 4),), jnp.float32),
        "second_pattern": picks_of(arg_keys[6], CB, CB, KEEP2, 0),
        "second_weight": centred(arg_keys[7], (CB, KEEP2, BLOCK, BLOCK), (KEEP2 * BLOCK) ** -0.5, 0.125, ((0, 4),)),
        "cotangent": centred(arg_keys[8], (BATCH, H), (BATCH ** -0.5), 0.09375, ((0, 8), (1, 4))),
    }


def silu_slope(v):
    s = jax.nn.sigmoid(v)
    return s * (1.0 + v * (1.0 - s))


def reference(reservoir, pull_list, pull_counts, first_pattern, first_weight, first_bias, second_pattern, second_weight, cotangent):
    slots = N_DP * CAP
    slot = jnp.arange(slots, dtype=jnp.int32)
    owner = slot // CAP
    within = slot % CAP
    counts = pull_counts.astype(jnp.int32)
    prefix = (jnp.cumsum(counts, axis=1).astype(jnp.int32) - counts).astype(jnp.int32)
    dest = jnp.where(within[None, :] < counts[:, owner], prefix[:, owner] + within[None, :], -1)
    global_ids = owner[None, :] * OWN + pull_list.reshape(N_DP, slots).astype(jnp.int32)
    match = dest[:, None, :] == jnp.arange(BLK_DEV, dtype=jnp.int32)[None, :, None]
    chosen = jnp.sum(jnp.where(match, global_ids[:, None, :], 0), axis=2).astype(jnp.int32)
    stored = reservoir.reshape(N_DP * OWN, BLOCK, DIN)
    w1 = first_weight.astype(jnp.float32)
    w2 = second_weight.astype(jnp.float32)
    bias = first_bias.reshape(CB, BLOCK)
    cbm = CB // N_MP
    upstream_all = cotangent.reshape(N_DP, ROWS, CB, BLOCK)

    def group(carry, xs):
        acc1, acc2, accb = carry
        picks, upstream = xs
        inputs = stored[picks].reshape(ROWS, IB1, BLOCK)
        picked1 = inputs[:, first_pattern].astype(jnp.float32)
        pre = jnp.einsum('rckf,ckfg->rcg', picked1, w1) + bias
        hidden = jax.nn.silu(pre).astype(jnp.bfloat16)
        picked2 = hidden[:, second_pattern].astype(jnp.float32)
        out = jnp.einsum('rckf,ckfg->rcg', picked2, w2).astype(jnp.bfloat16)
        up = upstream.astype(jnp.float32)
        part2 = jnp.einsum('rckf,rcg->ckfg', picked2, up).astype(jnp.bfloat16).astype(jnp.float32)
        contrib = jnp.einsum('rcg,ckfg->rckf', up, w2)

        def share(m):
            piece = lax.dynamic_slice_in_dim(contrib, m * cbm, cbm, 1)
            where = lax.dynamic_slice_in_dim(second_pattern, m * cbm, cbm, 0)
            total = jnp.zeros((ROWS, CB, BLOCK), jnp.float32).at[:, where].add(piece)
            return total.astype(jnp.bfloat16).astype(jnp.float32)

        hidden_grad = jnp.sum(lax.map(share, jnp.arange(N_MP, dtype=jnp.int32)), axis=0)
        pre_grad = (hidden_grad * silu_slope(pre)).astype(jnp.bfloat16).astype(jnp.float32)
        part1 = jnp.einsum('rckf,rcg->ckfg', picked1, pre_grad).astype(jnp.bfloat16).astype(jnp.float32)
        accb = accb + jnp.sum(pre_grad, axis=0)
        return (acc1 + part1, acc2 + part2, accb), out

    init = (jnp.zeros((CB, KEEP1, BLOCK, BLOCK), jnp.float32), jnp.zeros((CB, KEEP2, BLOCK, BLOCK), jnp.float32), jnp.zeros((CB, BLOCK), jnp.float32))
    (acc1, acc2, accb), outs = lax.scan(group, init, (chosen, upstream_all))
    second_out = outs.reshape(BATCH, H)
    return second_out, acc1.reshape(CB, KEEP1 * BLOCK * BLOCK), acc2.reshape(CB, KEEP2 * BLOCK * BLOCK), accb.reshape(H)
```

```python
import functools

import jax
import jax.numpy as jnp
from jax import lax
from jax.experimental import pallas as pl
from jax.experimental.pallas import tpu as pltpu
from jax.sharding import PartitionSpec as P

BF16 = jnp.bfloat16
F32 = jnp.float32


def params(mib):
    return pltpu.CompilerParams(vmem_limit_bytes=mib * 2**20)


def cost(flops, moved, trans=0):
    return pl.CostEstimate(flops=flops, bytes_accessed=moved, transcendentals=trans)


def dot(a, b):
    return jnp.dot(a, b, preferred_element_type=F32)


def pick_kernel(picks, stored, out):
    out[...] = stored[...]


def pick_blocks(picks, stored):
    slots, (_, side, width) = picks.shape[0], stored.shape
    return pl.pallas_call(
        pick_kernel,
        out_shape=jax.ShapeDtypeStruct((slots, side, width), stored.dtype),
        grid_spec=pltpu.PrefetchScalarGridSpec(
            num_scalar_prefetch=1,
            grid=(slots,),
            in_specs=[pl.BlockSpec((1, side, width), lambda i, p: (p[i], 0, 0))],
            out_specs=pl.BlockSpec((1, side, width), lambda i, p: (i, 0, 0)),
        ),
        name="pick",
    )(picks, stored)


def term_kernel(pattern, up, weight, out, acc):
    c = pl.program_id(0)
    keep, side = weight.shape[1], weight.shape[2]

    @pl.when(c == 0)
    def _():
        @pl.loop(0, acc.shape[0])
        def _(b):
            acc[b] = jnp.zeros(acc.shape[1:], F32)

    u = up[...]
    for k in range(0, keep, 2):
        pair = weight[0, k : k + 2].reshape(2 * side, side)
        spread = lax.dot_general(
            u, pair, (((1,), (1,)), ((), ())), preferred_element_type=F32
        )
        acc[pattern[c * keep + k]] += spread[:, :side]
        acc[pattern[c * keep + k + 1]] += spread[:, side:]

    @pl.when(c == pl.num_programs(0) - 1)
    def _():
        @pl.loop(0, acc.shape[0])
        def _(b):
            out[b] = acc[b].astype(BF16)


def hidden_term(pattern, cotangent, weight, all_blocks):
    cols, keep, side, _ = weight.shape
    rows = cotangent.shape[0]
    return pl.pallas_call(
        term_kernel,
        out_shape=jax.ShapeDtypeStruct((all_blocks, rows, side), BF16),
        grid_spec=pltpu.PrefetchScalarGridSpec(
            num_scalar_prefetch=1,
            grid=(cols,),
            in_specs=[
                pl.BlockSpec((rows, side), lambda c, p: (0, c)),
                pl.BlockSpec((1, keep, side, side), lambda c, p: (c, 0, 0, 0)),
            ],
            out_specs=pl.BlockSpec(
                (all_blocks, rows, side), lambda c, p: (0, 0, 0), pipeline_mode=pl.Buffered(1)
            ),
            scratch_shapes=[pltpu.VMEM((all_blocks, rows, side), F32)],
        ),
        compiler_params=params(40),
        cost_estimate=cost(2 * rows * cols * keep * side * side, 18 * 2**20),
        name="term",
    )(pattern.reshape(-1), cotangent, weight)


def first_kernel(
    pattern, source, got, weight, bias, part, hidden, hidden_t, grad, bias_part, x, xt
):
    step = pl.program_id(0)
    here, side = bias.shape[0], bias.shape[2]
    keep = weight.shape[0] * weight.shape[2] // (here * side)
    rows = x.shape[1]
    whole = weight[...].reshape(here, keep * side, side)

    @pl.when(step == 0)
    def _():
        for f in range(x.shape[0]):
            for j in range(rows // side):
                block = got[source[j], :, f * side : (f + 1) * side]
                x[f, j * side : (j + 1) * side, :] = block
                xt[f, :, j * side : (j + 1) * side] = block.T

    for i in range(here):
        at = [pattern[(step * here + i) * keep + k] for k in range(keep)]
        lhs = jnp.concatenate([x[a] for a in at], axis=1)
        v = dot(lhs, whole[i]) + bias[i]
        s = 1.0 / (1.0 + jnp.exp(-v))
        h = (v * s).astype(BF16)
        hidden[i] = h
        hidden_t[i] = h.T
        g = part[i].astype(F32) * (s * (1.0 + v * (1.0 - s)))
        bias_part[i] = jnp.sum(g, axis=0, keepdims=True)
        lhs_t = jnp.concatenate([xt[a] for a in at], axis=0)
        fg = dot(lhs_t, g.astype(BF16)).astype(BF16)
        grad[:, 0, i] = fg.reshape(grad.shape[0], -1, side)


def first_layer(pattern, source, got, weight, bias, part, n_mp, n_dp):
    blocks, keep = pattern.shape
    slots, side, width = got.shape
    rows = part.shape[1]
    local = blocks // n_mp
    here = 4 if local % 4 == 0 else 1
    per = local // here
    piece = keep * side // n_dp
    share = weight.shape[2]
    return pl.pallas_call(
        first_kernel,
        out_shape=(
            jax.ShapeDtypeStruct((blocks, rows, side), BF16),
            jax.ShapeDtypeStruct((blocks, side, rows), BF16),
            jax.ShapeDtypeStruct((n_dp, n_mp, local, piece, side), BF16),
            jax.ShapeDtypeStruct((blocks, 1, side), F32),
        ),
        grid_spec=pltpu.PrefetchScalarGridSpec(
            num_scalar_prefetch=2,
            grid=(blocks // here,),
            in_specs=[
                pl.BlockSpec(
                    (slots, side, width), lambda c, p, s: (0, 0, 0), pipeline_mode=pl.Buffered(1)
                ),
                pl.BlockSpec(
                    (n_dp // per, 1, share, side), lambda c, p, s: (c % per, c // per, 0, 0)
                ),
                pl.BlockSpec((here, 1, side), lambda c, p, s: (c, 0, 0)),
                pl.BlockSpec((here, rows, side), lambda c, p, s: (c, 0, 0)),
            ],
            out_specs=[
                pl.BlockSpec((here, rows, side), lambda c, p, s: (c, 0, 0)),
                pl.BlockSpec((here, side, rows), lambda c, p, s: (c, 0, 0)),
                pl.BlockSpec(
                    (n_dp, 1, here, piece, side), lambda c, p, s: (0, c // per, c % per, 0, 0)
                ),
                pl.BlockSpec((here, 1, side), lambda c, p, s: (c, 0, 0)),
            ],
            scratch_shapes=[
                pltpu.VMEM((width // side, rows, side), BF16),
                pltpu.VMEM((width // side, side, rows), BF16),
            ],
        ),
        compiler_params=params(32),
        cost_estimate=cost(4 * rows * blocks * keep * side * side, 30 * 2**20, 2**22),
        name="first",
    )(pattern.reshape(-1), source, got, weight, bias.reshape(blocks, 1, side), part)


def grad_kernel(pattern, hidden_t, up, out):
    c = pl.program_id(0)
    n, _, piece, side = out.shape
    keep = n * piece // side
    lhs = jnp.concatenate([hidden_t[pattern[c * keep + k]] for k in range(keep)], axis=0)
    out[:, 0] = dot(lhs, up[...]).astype(BF16).reshape(n, piece, side)


def second_gradient(pattern, hidden_t, cotangent, n_dp):
    cols, keep = pattern.shape
    blocks, side, rows = hidden_t.shape
    piece = keep * side // n_dp
    return pl.pallas_call(
        grad_kernel,
        out_shape=jax.ShapeDtypeStruct((n_dp, cols, piece, side), BF16),
        grid_spec=pltpu.PrefetchScalarGridSpec(
            num_scalar_prefetch=1,
            grid=(cols,),
            in_specs=[
                pl.BlockSpec(
                    (blocks, side, rows), lambda c, p: (0, 0, 0), pipeline_mode=pl.Buffered(1)
                ),
                pl.BlockSpec((rows, side), lambda c, p: (0, c)),
            ],
            out_specs=pl.BlockSpec((n_dp, 1, piece, side), lambda c, p: (0, c, 0, 0)),
        ),
        compiler_params=params(32),
        cost_estimate=cost(2 * rows * cols * keep * side * side, 18 * 2**20),
        name="second_grad",
    )(pattern.reshape(-1), hidden_t, cotangent)


def out_kernel(pattern, hidden, weight, out):
    c = pl.program_id(0)
    keep, side = weight.shape[1], weight.shape[2]
    lhs = jnp.concatenate([hidden[pattern[c * keep + k]] for k in range(keep)], axis=1)
    out[...] = dot(lhs, weight[0].reshape(keep * side, side)).astype(BF16)


def second_layer(pattern, hidden, weight):
    cols, keep, side, _ = weight.shape
    blocks, rows, _ = hidden.shape
    return pl.pallas_call(
        out_kernel,
        out_shape=jax.ShapeDtypeStruct((rows, cols * side), BF16),
        grid_spec=pltpu.PrefetchScalarGridSpec(
            num_scalar_prefetch=1,
            grid=(cols,),
            in_specs=[
                pl.BlockSpec(
                    (blocks, rows, side), lambda c, p: (0, 0, 0), pipeline_mode=pl.Buffered(1)
                ),
                pl.BlockSpec((1, keep, side, side), lambda c, p: (c, 0, 0, 0)),
            ],
            out_specs=pl.BlockSpec((rows, side), lambda c, p: (0, c)),
        ),
        compiler_params=params(32),
        cost_estimate=cost(2 * rows * cols * keep * side * side, 18 * 2**20),
        name="second_out",
    )(pattern.reshape(-1), hidden, weight)


def body(
    reservoir,
    pull_list,
    pull_counts,
    first_pattern,
    first_weight,
    first_bias,
    second_pattern,
    second_weight,
    cotangent,
):
    n_dp, n_mp = lax.axis_size("dp"), lax.axis_size("mp")
    d = lax.axis_index("dp")
    local, keep1, side, _ = first_weight.shape
    keep2 = second_weight.shape[1]
    width_in = reservoir.shape[1]
    cap = pull_list.shape[2]
    rows = cotangent.shape[0]
    slots = n_dp * cap
    blocks = local * n_mp

    stored = reservoir.reshape(-1, side, width_in)
    sending = pick_blocks(pull_list[:, 0, :].reshape(slots), stored)
    got = lax.all_to_all(sending, "dp", split_axis=0, concat_axis=0, tiled=True)

    flat = first_weight.reshape(-1, side)
    share = flat.shape[0] // n_dp
    mine = lax.dynamic_slice_in_dim(flat, d * share, share, 0)
    weight = lax.all_gather(mine, "mp", axis=0, tiled=True)
    weight = lax.all_gather(weight, "dp", axis=0, tiled=True)
    weight = weight.reshape(n_dp, n_mp, share, side)
    small = jnp.concatenate([first_bias, first_pattern.astype(F32).reshape(-1)])
    small = lax.all_gather(small, "mp", axis=0)
    bias = small[:, : local * side].reshape(blocks, side)
    pattern1 = small[:, local * side :].astype(jnp.int32).reshape(blocks, keep1)

    counts = pull_counts[0]
    position = jnp.arange(slots, dtype=jnp.int32)
    owner, within = position // cap, position % cap
    prefix = jnp.cumsum(counts) - counts
    dest = jnp.where(within < counts[owner], prefix[owner] + within, -1)
    match = dest[None, :] == jnp.arange(rows // side, dtype=jnp.int32)[:, None]
    source = jnp.sum(jnp.where(match, position[None, :], 0), axis=1).astype(jnp.int32)

    part = hidden_term(second_pattern, cotangent, second_weight, blocks)
    hidden, hidden_t, grad1, bias_part = first_layer(
        pattern1, source, got, weight, bias, part, n_mp, n_dp
    )
    grad1 = lax.psum_scatter(
        grad1.reshape(n_dp, -1, side), "dp", scatter_dimension=0, tiled=True
    )
    grad1 = lax.psum_scatter(
        grad1.reshape(n_mp, -1, side), "mp", scatter_dimension=0, tiled=True
    )
    grad2 = second_gradient(second_pattern, hidden_t, cotangent, n_dp)
    grad2 = lax.psum_scatter(
        grad2.reshape(n_dp, -1, side), "dp", scatter_dimension=0, tiled=True
    )
    second_out = second_layer(second_pattern, hidden, second_weight)
    bias_all = lax.psum(bias_part.reshape(n_mp, local * side), ("mp", "dp"))
    bias_grad = lax.dynamic_index_in_dim(bias_all, lax.axis_index("mp"), 0, keepdims=False)
    return (
        second_out,
        grad1.reshape(local, -1).astype(F32),
        grad2.reshape(local, -1).astype(F32),
        bias_grad,
    )


def solution(mesh):
    return jax.shard_map(
        body,
        mesh=mesh,
        in_specs=(
            P("dp", None),
            P(None, "dp", None),
            P("dp", None),
            P("mp", None),
            P("mp", None, None, None),
            P("mp"),
            P("mp", None),
            P("mp", None, None, None),
            P("dp", "mp"),
        ),
        out_specs=(P("dp", "mp"), P("mp", "dp"), P("mp", "dp"), P("mp")),
        check_vma=False,
    )
```

```python
import functools

import jax
import jax.numpy as jnp
from jax import lax
from jax.experimental import pallas as pl
from jax.experimental.pallas import tpu as pltpu
from jax.sharding import PartitionSpec as P

BF16 = jnp.bfloat16
F32 = jnp.float32


def params(mib):
    return pltpu.CompilerParams(vmem_limit_bytes=mib * 2**20)


def cost(flops, moved, trans=0):
    return pl.CostEstimate(flops=flops, bytes_accessed=moved, transcendentals=trans)


def dot(a, b):
    return jnp.dot(a, b, preferred_element_type=F32)


def pick_kernel(picks, stored, out):
    out[...] = stored[...]


def pick_blocks(picks, stored):
    slots, (_, side, width) = picks.shape[0], stored.shape
    return pl.pallas_call(
        pick_kernel,
        out_shape=jax.ShapeDtypeStruct((slots, side, width), stored.dtype),
        grid_spec=pltpu.PrefetchScalarGridSpec(
            num_scalar_prefetch=1,
            grid=(slots,),
            in_specs=[pl.BlockSpec((1, side, width), lambda i, p: (p[i], 0, 0))],
            out_specs=pl.BlockSpec((1, side, width), lambda i, p: (i, 0, 0)),
        ),
        name="pick",
    )(picks, stored)


def term_kernel(pattern, up, weight, out, acc):
    c = pl.program_id(0)
    keep, side = weight.shape[1], weight.shape[2]

    @pl.when(c == 0)
    def _():
        @pl.loop(0, acc.shape[0])
        def _(b):
            acc[b] = jnp.zeros(acc.shape[1:], F32)

    u = up[...]
    for k in range(0, keep, 2):
        pair = weight[0, k : k + 2].reshape(2 * side, side)
        spread = lax.dot_general(
            u, pair, (((1,), (1,)), ((), ())), preferred_element_type=F32
        )
        acc[pattern[c * keep + k]] += spread[:, :side]
        acc[pattern[c * keep + k + 1]] += spread[:, side:]

    @pl.when(c == pl.num_programs(0) - 1)
    def _():
        @pl.loop(0, acc.shape[0])
        def _(b):
            out[b] = acc[b].astype(BF16)


def hidden_term(pattern, cotangent, weight, all_blocks):
    cols, keep, side, _ = weight.shape
    rows = cotangent.shape[0]
    return pl.pallas_call(
        term_kernel,
        out_shape=jax.ShapeDtypeStruct((all_blocks, rows, side), BF16),
        grid_spec=pltpu.PrefetchScalarGridSpec(
            num_scalar_prefetch=1,
            grid=(cols,),
            in_specs=[
                pl.BlockSpec((rows, side), lambda c, p: (0, c)),
                pl.BlockSpec((1, keep, side, side), lambda c, p: (c, 0, 0, 0)),
            ],
            out_specs=pl.BlockSpec(
                (all_blocks, rows, side), lambda c, p: (0, 0, 0), pipeline_mode=pl.Buffered(1)
            ),
            scratch_shapes=[pltpu.VMEM((all_blocks, rows, side), F32)],
        ),
        compiler_params=params(40),
        cost_estimate=cost(2 * rows * cols * keep * side * side, 18 * 2**20),
        name="term",
    )(pattern.reshape(-1), cotangent, weight)


def first_kernel(
    pattern, source, got, weight, bias, part, hidden, hidden_t, grad, bias_part, x, xt
):
    step = pl.program_id(0)
    here, side = bias.shape[0], bias.shape[2]
    keep = weight.shape[0] * weight.shape[2] // (here * side)
    rows = x.shape[1]
    whole = weight[...].reshape(here, keep * side, side)

    @pl.when(step == 0)
    def _():
        for f in range(x.shape[0]):
            for j in range(rows // side):
                block = got[source[j], :, f * side : (f + 1) * side]
                x[f, j * side : (j + 1) * side, :] = block
                xt[f, :, j * side : (j + 1) * side] = block.T

    for i in range(here):
        at = [pattern[(step * here + i) * keep + k] for k in range(keep)]
        lhs = jnp.concatenate([x[a] for a in at], axis=1)
        v = dot(lhs, whole[i]) + bias[i]
        s = 1.0 / (1.0 + jnp.exp(-v))
        h = (v * s).astype(BF16)
        hidden[i] = h
        hidden_t[i] = h.T
        g = part[i].astype(F32) * (s * (1.0 + v * (1.0 - s)))
        bias_part[i] = jnp.sum(g, axis=0, keepdims=True)
        lhs_t = jnp.concatenate([xt[a] for a in at], axis=0)
        fg = dot(lhs_t, g.astype(BF16)).astype(BF16)
        piece = keep * side // grad.shape[0]
        grad[:, i * piece : (i + 1) * piece] = fg.reshape(-1, piece, side)


def first_layer(pattern, source, got, weight, bias, part, n_mp, n_dp, extra):
    blocks, keep = pattern.shape
    slots, side, width = got.shape
    rows = part.shape[1]
    local = blocks // n_mp
    here = 4 if local % 4 == 0 else 1
    per = local // here
    piece = keep * side // n_dp
    share = weight.shape[2]
    return pl.pallas_call(
        first_kernel,
        out_shape=(
            jax.ShapeDtypeStruct((blocks, rows, side), BF16),
            jax.ShapeDtypeStruct((blocks, side, rows), BF16),
            jax.ShapeDtypeStruct((n_dp, blocks * piece + extra, side), BF16),
            jax.ShapeDtypeStruct((blocks, 1, side), F32),
        ),
        grid_spec=pltpu.PrefetchScalarGridSpec(
            num_scalar_prefetch=2,
            grid=(blocks // here,),
            in_specs=[
                pl.BlockSpec(
                    (slots, side, width), lambda c, p, s: (0, 0, 0), pipeline_mode=pl.Buffered(1)
                ),
                pl.BlockSpec(
                    (n_dp // per, 1, share, side), lambda c, p, s: (c % per, c // per, 0, 0)
                ),
                pl.BlockSpec((here, 1, side), lambda c, p, s: (c, 0, 0)),
                pl.BlockSpec((here, rows, side), lambda c, p, s: (c, 0, 0)),
            ],
            out_specs=[
                pl.BlockSpec((here, rows, side), lambda c, p, s: (c, 0, 0)),
                pl.BlockSpec((here, side, rows), lambda c, p, s: (c, 0, 0)),
                pl.BlockSpec((n_dp, here * piece, side), lambda c, p, s: (0, c, 0)),
                pl.BlockSpec((here, 1, side), lambda c, p, s: (c, 0, 0)),
            ],
            scratch_shapes=[
                pltpu.VMEM((width // side, rows, side), BF16),
                pltpu.VMEM((width // side, side, rows), BF16),
            ],
        ),
        compiler_params=params(32),
        cost_estimate=cost(4 * rows * blocks * keep * side * side, 30 * 2**20, 2**22),
        name="first",
    )(pattern.reshape(-1), source, got, weight, bias.reshape(blocks, 1, side), part)


def grad_kernel(pattern, hidden_t, up, both, out):
    c = pl.program_id(0)
    n, piece, side = out.shape
    keep = n * piece // side
    lhs = jnp.concatenate([hidden_t[pattern[c * keep + k]] for k in range(keep)], axis=0)
    out[...] = dot(lhs, up[...]).astype(BF16).reshape(n, piece, side)


def second_gradient(pattern, hidden_t, cotangent, both):
    cols, keep = pattern.shape
    blocks, side, rows = hidden_t.shape
    n_dp, total, _ = both.shape
    piece = keep * side // n_dp
    skip = total // piece - cols
    return pl.pallas_call(
        grad_kernel,
        out_shape=jax.ShapeDtypeStruct(both.shape, BF16),
        grid_spec=pltpu.PrefetchScalarGridSpec(
            num_scalar_prefetch=1,
            grid=(cols,),
            in_specs=[
                pl.BlockSpec(
                    (blocks, side, rows), lambda c, p: (0, 0, 0), pipeline_mode=pl.Buffered(1)
                ),
                pl.BlockSpec((rows, side), lambda c, p: (0, c)),
                pl.BlockSpec(memory_space=pl.ANY),
            ],
            out_specs=pl.BlockSpec((n_dp, piece, side), lambda c, p: (0, skip + c, 0)),
        ),
        input_output_aliases={3: 0},
        compiler_params=params(32),
        cost_estimate=cost(2 * rows * cols * keep * side * side, 18 * 2**20),
        name="second_grad",
    )(pattern.reshape(-1), hidden_t, cotangent, both)


def out_kernel(pattern, hidden, weight, out):
    c = pl.program_id(0)
    keep, side = weight.shape[1], weight.shape[2]
    lhs = jnp.concatenate([hidden[pattern[c * keep + k]] for k in range(keep)], axis=1)
    out[...] = dot(lhs, weight[0].reshape(keep * side, side)).astype(BF16)


def second_layer(pattern, hidden, weight):
    cols, keep, side, _ = weight.shape
    blocks, rows, _ = hidden.shape
    return pl.pallas_call(
        out_kernel,
        out_shape=jax.ShapeDtypeStruct((rows, cols * side), BF16),
        grid_spec=pltpu.PrefetchScalarGridSpec(
            num_scalar_prefetch=1,
            grid=(cols,),
            in_specs=[
                pl.BlockSpec(
                    (blocks, rows, side), lambda c, p: (0, 0, 0), pipeline_mode=pl.Buffered(1)
                ),
                pl.BlockSpec((1, keep, side, side), lambda c, p: (c, 0, 0, 0)),
            ],
            out_specs=pl.BlockSpec((rows, side), lambda c, p: (0, c)),
        ),
        compiler_params=params(32),
        cost_estimate=cost(2 * rows * cols * keep * side * side, 18 * 2**20),
        name="second_out",
    )(pattern.reshape(-1), hidden, weight)


def body(
    reservoir,
    pull_list,
    pull_counts,
    first_pattern,
    first_weight,
    first_bias,
    second_pattern,
    second_weight,
    cotangent,
):
    n_dp, n_mp = lax.axis_size("dp"), lax.axis_size("mp")
    d = lax.axis_index("dp")
    local, keep1, side, _ = first_weight.shape
    keep2 = second_weight.shape[1]
    width_in = reservoir.shape[1]
    cap = pull_list.shape[2]
    rows = cotangent.shape[0]
    slots = n_dp * cap
    blocks = local * n_mp

    stored = reservoir.reshape(-1, side, width_in)
    sending = pick_blocks(pull_list[:, 0, :].reshape(slots), stored)
    got = lax.all_to_all(sending, "dp", split_axis=0, concat_axis=0, tiled=True)

    flat = first_weight.reshape(-1, side)
    share = flat.shape[0] // n_dp
    mine = lax.dynamic_slice_in_dim(flat, d * share, share, 0)
    weight = lax.all_gather(mine, "mp", axis=0, tiled=True)
    weight = lax.all_gather(weight, "dp", axis=0, tiled=True)
    weight = weight.reshape(n_dp, n_mp, share, side)
    small = jnp.concatenate([first_bias, first_pattern.astype(F32).reshape(-1)])
    small = lax.all_gather(small, "mp", axis=0)
    bias = small[:, : local * side].reshape(blocks, side)
    pattern1 = small[:, local * side :].astype(jnp.int32).reshape(blocks, keep1)

    counts = pull_counts[0]
    position = jnp.arange(slots, dtype=jnp.int32)
    owner, within = position // cap, position % cap
    prefix = jnp.cumsum(counts) - counts
    dest = jnp.where(within < counts[owner], prefix[owner] + within, -1)
    match = dest[None, :] == jnp.arange(rows // side, dtype=jnp.int32)[:, None]
    source = jnp.sum(jnp.where(match, position[None, :], 0), axis=1).astype(jnp.int32)

    part = hidden_term(second_pattern, cotangent, second_weight, blocks)
    extra = local * keep2 * side // n_dp
    hidden, hidden_t, both, bias_part = first_layer(
        pattern1, source, got, weight, bias, part, n_mp, n_dp, extra
    )
    both = second_gradient(second_pattern, hidden_t, cotangent, both)
    both = lax.psum_scatter(both, "dp", scatter_dimension=0, tiled=True)[0]
    head = both.shape[0] - extra
    grad1 = lax.all_to_all(
        both[:head].reshape(n_mp, -1, side), "mp", split_axis=0, concat_axis=0, tiled=True
    )
    grad1 = jnp.sum(grad1.astype(F32), axis=0)
    grad2 = both[head:]
    second_out = second_layer(second_pattern, hidden, second_weight)
    bias_all = lax.psum(bias_part.reshape(n_mp, local * side), ("mp", "dp"))
    bias_grad = lax.dynamic_index_in_dim(bias_all, lax.axis_index("mp"), 0, keepdims=False)
    return (
        second_out,
        grad1.reshape(local, -1),
        grad2.reshape(local, -1).astype(F32),
        bias_grad,
    )


def solution(mesh):
    return jax.shard_map(
        body,
        mesh=mesh,
        in_specs=(
            P("dp", None),
            P(None, "dp", None),
            P("dp", None),
            P("mp", None),
            P("mp", None, None, None),
            P("mp"),
            P("mp", None),
            P("mp", None, None, None),
            P("dp", "mp"),
        ),
        out_specs=(P("dp", "mp"), P("mp", "dp"), P("mp", "dp"), P("mp")),
        check_vma=False,
    )
```
